512 devices in a mesh: section: 8 (over z), tok: 64 (over y, x, core).
Axes of the slice: x: 4, y: 8, z: 8, core: 2. Of those that a mesh axis runs over, the one named last changes fastest.
Arguments:
- queries: bfloat16 [8, 16384, 4096], P('section', 'tok'), may hold values from -120 to 120
- suffix_kv: bfloat16 [8, 16384, 1024], P('section', 'tok'), may hold values from -4 to 4
- prefix_kv: bfloat16 [8, 64, 64, 1024], P('section', 'tok'), may hold values from -4 to 4
- served: int32 [8, 128, 8], P('section'), may hold values from -1 to 63, as said below
Outputs:
- passed: bfloat16 [8, 16384, 4096], P('section', 'tok')
The draws below stay inside these ranges and needn't reach their ends.
Inputs may be any that keep to these rules, and one draw needn't show every extreme that they name: `served`: entry k of a row is -1 or a page in [k * 8, (k + 1) * 8); live entries come first, then -1; entry 0 is always live, and block 0 of every section has all 8 live.
All inputs are finite; a program needn't handle non-finite values.
Results may differ from the reference program's by a relative error of at most 0.0029.
Values may be sent and summed in bfloat16 or wider, within the bound.
No kernel may reach another device: no remote copies, remote signals or barrier semaphores. Data moves between devices by JAX's collectives and lax.ppermute only.
A program may use at most 64 MiB of HBM per device.

```python
import math
import jax
import jax.numpy as jnp
from jax import lax

Q_HEADS = 32
KV_HEADS = 4
HEAD = 128
BLOCK = 128
PAGE = 64
DEPTH = 8
PB = 64
WIDE = 8
QB = 128
N_SECTION = 8


def joint_draw(key):
    base_key = jax.random.fold_in(key, 11)
    key_query, key_pairs = jax.random.split(base_key)
    pair_shape = (N_SECTION, QB, BLOCK, 2 * KV_HEADS * HEAD)
    query_shape = (N_SECTION, QB, BLOCK, Q_HEADS * HEAD)
    pairs = jnp.clip(jax.random.normal(key_pairs, pair_shape, jnp.float32), -4.0, 4.0)
    query_vals = jnp.clip(2.5 * jax.random.normal(key_query, query_shape, jnp.float32), -10.0, 10.0)
    query_vals = query_vals.reshape(N_SECTION, QB * BLOCK, Q_HEADS * HEAD)
    pairs = pairs.reshape(N_SECTION, QB * BLOCK, 2 * KV_HEADS * HEAD)
    return (query_vals, pairs)


def draw_queries(key, part):
    return joint_draw(key)[0].astype(jnp.bfloat16)


def draw_suffix_kv(key, part):
    return joint_draw(key)[1].astype(jnp.bfloat16)


def draw_served(key, part):
    key_pick, key_count = jax.random.split(jax.random.fold_in(key, 5))
    offsets = (jnp.arange(DEPTH) * WIDE).astype(jnp.int32)
    picks = jax.random.randint(key_pick, (N_SECTION, QB, DEPTH), 0, WIDE).astype(jnp.int32) + offsets
    counts = jax.random.randint(key_count, (N_SECTION, QB, 1), 1, DEPTH + 1).astype(jnp.int32)
    counts = counts.at[:, 0, :].set(DEPTH)
    slot_pos = lax.broadcasted_iota(jnp.int32, (N_SECTION, QB, DEPTH), 2)
    return jnp.where(slot_pos < counts, picks, -1).astype(jnp.int32)


def level_of(key, extent, shards, least, top_value):
    def one(axis_at, blocks):
        steps = jax.random.uniform(jax.random.fold_in(jax.random.fold_in(key, 6), axis_at), (blocks,), jnp.float32, least / len(shards), top_value / len(shards))
        return jnp.repeat(jnp.exp(steps), extent[axis_at] // blocks).reshape((-1,) + (1,) * (len(extent) - axis_at - 1))

    level = one(*shards[0])
    for cut in shards[1:]:
        level = level * one(*cut)
    return level


def noise(stream_key, shape, spread, most, cuts=(), dtype=jnp.bfloat16):
    level = level_of(stream_key, shape, cuts, -0.22, 0.18) if cuts else 1.0
    entries = jax.random.normal(stream_key, shape, jnp.float32) * spread * level
    return jnp.minimum(jnp.maximum(entries, -most), most).astype(dtype)


def setup_inputs(seed: int = 0) -> dict:
    splits = jax.random.split(jax.random.key(seed), 5)
    queries = draw_queries(jax.random.fold_in(splits[4], 71), 0)
    suffix_kv = draw_suffix_kv(jax.random.fold_in(splits[4], 71), 0)
    prefix_kv = noise(splits[2], (N_SECTION, PB, PAGE, 2 * KV_HEADS * HEAD), 1.0, 4.0, ((0, 8), (1, 64)))
    served = draw_served(jax.random.fold_in(splits[4], 71), 0)
    return dict(queries=queries, suffix_kv=suffix_kv, prefix_kv=prefix_kv, served=served)


def attend(query_rows, key_rows, value_rows, allowed, score_scale):
    scores = jnp.einsum('qgd,kd->gqk', query_rows.astype(jnp.float32), key_rows.astype(jnp.float32)) * score_scale
    scores = jnp.where(allowed[None], scores, -jnp.inf)
    row_top = lax.optimization_barrier(jnp.max(scores, axis=2, keepdims=True))
    exponent = jnp.exp(scores - row_top)
    totals = lax.optimization_barrier(jnp.sum(exponent, axis=2))
    weights = lax.optimization_barrier(exponent.astype(jnp.bfloat16)).astype(jnp.float32)
    mixture = jnp.einsum('gqk,kd->qgd', weights, value_rows.astype(jnp.float32))
    return (mixture / jnp.transpose(totals)[:, :, None]).astype(jnp.bfloat16)

def reference(queries, suffix_kv, prefix_kv, served):
    sections = queries.shape[0]
    group_size = Q_HEADS // KV_HEADS
    score_scale = 1.0 / math.sqrt(HEAD)
    query_blocks = queries.reshape(sections, QB, BLOCK, KV_HEADS, group_size, HEAD)
    own_pairs = suffix_kv.reshape(sections, QB, BLOCK, 2, KV_HEADS, HEAD)
    row_index = lax.broadcasted_iota(jnp.int32, (BLOCK, BLOCK), 0)
    col_index = lax.broadcasted_iota(jnp.int32, (BLOCK, BLOCK), 1)
    causal = col_index <= row_index

    def per_block(position):
        section_id = position // QB
        block_id = position % QB
        picks = served[section_id, block_id]
        prefix_pairs = prefix_kv[section_id][jnp.maximum(picks, 0)]
        prefix_pairs = prefix_pairs.reshape(DEPTH * PAGE, 2, KV_HEADS, HEAD)
        both_pairs = jnp.concatenate([prefix_pairs, own_pairs[section_id, block_id]], axis=0)
        live_rows = jnp.repeat(picks >= 0, PAGE)
        allowed = jnp.concatenate([jnp.broadcast_to(live_rows[None], (BLOCK, DEPTH * PAGE)), causal], axis=1)

        def per_head(query_rows, key_rows, value_rows):
            return attend(query_rows, key_rows, value_rows, allowed, score_scale)
        head_outputs = jax.vmap(per_head, in_axes=(1, 1, 1), out_axes=1)(query_blocks[section_id, block_id], both_pairs[:, 0], both_pairs[:, 1])
        return head_outputs.reshape(BLOCK, Q_HEADS * HEAD)
    blocks_out = lax.map(per_block, jnp.arange(sections * QB))
    attention = blocks_out.reshape(sections, QB * BLOCK, Q_HEADS * HEAD)
    return jnp.roll(attention, 1, axis=0)
```

```python
import functools
import math

import jax
import jax.numpy as jnp
from jax import lax
from jax.experimental import pallas as pl
from jax.experimental.pallas import tpu as pltpu
from jax.sharding import PartitionSpec as P


Q_HEADS = 32
KV_HEADS = 4
GROUP = Q_HEADS // KV_HEADS
HEAD = 128
BLOCK = 128
PAGE = 64
DEPTH = 8
QB_DEV = 2
ROWS, CHIPS, CORES = 8, 4, 2
ROW_DEV = CHIPS * CORES
KEYS = DEPTH * PAGE + BLOCK

A_CHUNKS = ((0, 1),)
B_HEADS = (2, 3)


SMEM = functools.partial(pl.BlockSpec, memory_space=pltpu.SMEM)
VMEM = functools.partial(pl.BlockSpec, memory_space=pltpu.VMEM)


def next_section(x):
    n = lax.axis_size("section")
    return lax.ppermute(x, "section", [(i, (i + 1) % n) for i in range(n)])


def within_tok(x, chips=0, cores=0):
    pairs = []
    for row in range(ROWS):
        for chip in range(CHIPS):
            for core in range(CORES):
                there = (row * CHIPS + (chip + chips) % CHIPS) * CORES + (core + cores) % CORES
                pairs.append(((row * CHIPS + chip) * CORES + core, there))
    return lax.ppermute(x, "tok", pairs)


def across_rows(x):
    columns = [[row * ROW_DEV + at for row in range(ROWS)] for at in range(ROW_DEV)]
    return lax.all_to_all(x, "tok", 0, 0, axis_index_groups=columns, tiled=True)


def columns_of(heads):
    width = len(heads) * HEAD
    starts = (heads[0] * HEAD, (KV_HEADS + heads[0]) * HEAD)
    return [(i * width, (i + 1) * width, start, start + width) for i, start in enumerate(starts)]


def copies_kernel(columns, page, out):
    for to, to_end, start, end in columns:
        part = page[:, start:end]
        for i in range(out.shape[0]):
            out[i, :, to:to_end] = part


def stack_kernel(columns, *refs):
    out = refs[-1]
    for i, page in enumerate(refs[:-1]):
        for to, to_end, start, end in columns:
            out[i, :, to:to_end] = page[:, start:end]


def small_kernel(body, out_shape, *args):
    return pl.pallas_call(
        body,
        out_shape=out_shape,
        in_specs=[VMEM()] * len(args),
        out_specs=VMEM(),
        compiler_params=pltpu.CompilerParams(vmem_limit_bytes=4 << 20),
        cost_estimate=pl.CostEstimate(flops=0, transcendentals=0, bytes_accessed=1 << 20),
    )(*args)


def slot_of(served, block, level):
    pick = jnp.clip(served[block, level] - level * ROW_DEV, 0, ROW_DEV - 1)
    return pick // CORES, pick % CORES


def pick_for_rows_kernel(tok, served, mine, other, out):
    at = tok[0] % ROW_DEV
    level = tok[0] // ROW_DEV
    chip, core = at // CORES, at % CORES

    def one(i, carry):
        row, b = i // QB_DEV, i % QB_DEV
        owner_chip, owner_core = slot_of(served, (row * ROW_DEV + at) * QB_DEV + b, level)
        back = (chip - owner_chip + CHIPS) % CHIPS

        @pl.when(owner_core == core)
        def _():
            out[row, b] = mine[back]

        @pl.when(owner_core != core)
        def _():
            out[row, b] = other[back]

        return carry

    lax.fori_loop(0, ROWS * QB_DEV, one, 0)


def pick_for_rows(tok, served, mine, other):
    width = mine.shape[-1]
    return pl.pallas_call(
        pick_for_rows_kernel,
        out_shape=jax.ShapeDtypeStruct((ROWS, QB_DEV, PAGE, width), mine.dtype),
        in_specs=[SMEM(), SMEM(), VMEM(), VMEM()],
        out_specs=VMEM(),
        compiler_params=pltpu.CompilerParams(vmem_limit_bytes=16 << 20),
        cost_estimate=pl.CostEstimate(flops=0, transcendentals=0, bytes_accessed=4 << 20),
        name="pick_for_rows",
    )(tok, served, mine, other)


def pick_for_pair_kernel(tok, served, from0, from1, from2, from3, own, send):
    chip = tok[0] % ROW_DEV // CORES
    sources = (from0, from1, from2, from3)
    for b in range(QB_DEV):
        for level in range(DEPTH):
            for whose, out in ((tok[0], own), (tok[0] // CORES * CORES + 1 - tok[0] % CORES, send)):
                owner_chip, _ = slot_of(served, whose * QB_DEV + b, level)
                back = (chip - owner_chip + CHIPS) % CHIPS
                for d, source in enumerate(sources):

                    @pl.when(back == d)
                    def _(d=d, source=source, out=out):
                        out[b, level] = source[level]


def pick_for_pair(tok, served, sources):
    shape = jax.ShapeDtypeStruct((QB_DEV,) + sources[0].shape, sources[0].dtype)
    return pl.pallas_call(
        pick_for_pair_kernel,
        out_shape=(shape, shape),
        in_specs=[SMEM(), SMEM()] + [VMEM()] * CHIPS,
        out_specs=(VMEM(), VMEM()),
        compiler_params=pltpu.CompilerParams(vmem_limit_bytes=16 << 20),
        cost_estimate=pl.CostEstimate(flops=0, transcendentals=0, bytes_accessed=8 << 20),
        name="pick_for_pair",
    )(tok, served, *sources)


def attend(queries, own_keys, own_values, out, keys, values):
    keys[DEPTH * PAGE :, :] = own_keys[...]
    values[DEPTH * PAGE :, :HEAD] = own_values[...]
    values[DEPTH * PAGE :, HEAD:] = jnp.ones((BLOCK, HEAD), jnp.bfloat16)
    to_exp2 = math.log2(math.e) / math.sqrt(HEAD)
    row_index = lax.broadcasted_iota(jnp.int32, (BLOCK, BLOCK), 0)
    col_index = lax.broadcasted_iota(jnp.int32, (BLOCK, BLOCK), 1)
    causal = col_index <= row_index
    for g in range(GROUP):
        scores = lax.dot_general(
            queries[:, g * HEAD : (g + 1) * HEAD],
            keys[...],
            (((1,), (1,)), ((), ())),
            preferred_element_type=jnp.float32,
        )
        own = jnp.where(causal, scores[:, DEPTH * PAGE :], -jnp.inf)
        scores = jnp.concatenate([scores[:, : DEPTH * PAGE], own], axis=1)
        top = jnp.max(scores, axis=1, keepdims=True)
        weights = jnp.exp2((scores - top) * to_exp2).astype(jnp.bfloat16)
        mixed = jnp.dot(weights, values[...], preferred_element_type=jnp.float32)
        out[:, g * HEAD : (g + 1) * HEAD] = (mixed[:, :HEAD] / mixed[:, HEAD:]).astype(out.dtype)


def attend_kernel(y_first, tok, served, *refs):
    if y_first:
        own_k, own_v, pair_k, pair_v, queries, own_keys, own_values = refs[:7]
    else:
        page_k, page_v, queries, own_keys, own_values = refs[:5]
    out, keys, values = refs[-3:]
    block = tok[0] * QB_DEV + pl.program_id(1)
    core = tok[0] % CORES

    def put(level, key_rows, value_rows):
        rows = slice(level * PAGE, (level + 1) * PAGE)
        keys[rows, :] = key_rows
        values[rows, :HEAD] = value_rows
        values[rows, HEAD:] = jnp.ones((PAGE, HEAD), jnp.bfloat16)

    for level in range(DEPTH):
        live = served[block, level] >= 0
        if y_first:
            here = slot_of(served, block, level)[1] == core

            @pl.when(live & here)
            def _(level=level):
                put(level, own_k[0, level], own_v[0, level])

            @pl.when(live & jnp.logical_not(here))
            def _(level=level):
                put(level, pair_k[0, level], pair_v[0, level])

        else:

            @pl.when(live)
            def _(level=level):
                put(level, page_k[level, 0], page_v[level, 0])

        @pl.when(jnp.logical_not(live))
        def _(level=level):
            rows = slice(level * PAGE, (level + 1) * PAGE)
            keys[rows, :] = keys[:PAGE, :]
            values[rows, :] = jnp.zeros((PAGE, 2 * HEAD), jnp.bfloat16)

    attend(queries, own_keys, own_values, out, keys, values)


def attention(tok, served, pages, heads, queries, own_pairs, result):
    y_first = len(pages) == 2
    count, first = len(heads), heads[0]
    if y_first:
        page_block = (1, DEPTH, PAGE, HEAD)
        at = lambda part: pl.BlockSpec(page_block, lambda h, b: (b, 0, 0, part * count + h))
    else:
        page_block = (DEPTH, 1, PAGE, HEAD)
        at = lambda part: pl.BlockSpec(page_block, lambda h, b: (0, b, 0, part * count + h))
    wide = pl.BlockSpec((BLOCK, GROUP * HEAD), lambda h, b: (b, first + h))
    own = lambda part: pl.BlockSpec((BLOCK, HEAD), lambda h, b: (b, part * KV_HEADS + first + h))
    page_args, page_specs = [], []
    for page in pages:
        page_args += [page, page]
        page_specs += [at(0), at(1)]
    args = [tok, served] + page_args + [queries, own_pairs, own_pairs]
    specs = [SMEM(), SMEM()] + page_specs + [wide, own(0), own(1)]
    aliases = {}
    if result is not None:
        aliases = {len(args): 0}
        args.append(result)
        specs.append(pl.BlockSpec(memory_space=pl.ANY))
    items = count * QB_DEV * GROUP * BLOCK * KEYS
    return pl.pallas_call(
        functools.partial(attend_kernel, y_first),
        grid=(count, QB_DEV),
        out_shape=jax.ShapeDtypeStruct(queries.shape, queries.dtype),
        in_specs=specs,
        out_specs=wide,
        scratch_shapes=[pltpu.VMEM((KEYS, HEAD), jnp.bfloat16), pltpu.VMEM((KEYS, 2 * HEAD), jnp.bfloat16)],
        input_output_aliases=aliases,
        compiler_params=pltpu.CompilerParams(vmem_limit_bytes=24 << 20),
        cost_estimate=pl.CostEstimate(flops=items * 6 * HEAD, transcendentals=items, bytes_accessed=4 << 20),
        name="attend_b" if y_first else "attend_a",
    )(*args)


def on_device(queries, suffix_kv, prefix_kv, served):
    tok = lax.axis_index("tok").reshape(1)
    page = next_section(prefix_kv[0, 0])
    served = next_section(served[0])
    own_pairs = next_section(suffix_kv[0])
    queries = next_section(queries[0])

    def chip_copies(x):
        copies = [x]
        for d in range(1, CHIPS):
            copies.append(within_tok(x, chips=d))
        return copies

    width = 2 * len(B_HEADS) * HEAD
    level_b = small_kernel(
        functools.partial(copies_kernel, columns_of(B_HEADS)),
        jax.ShapeDtypeStruct((ROWS, PAGE, width), page.dtype),
        page,
    )
    level_b = across_rows(level_b)

    row_pages = chip_copies(page)
    a_heads = sum(A_CHUNKS, ())
    width = 2 * len(a_heads) * HEAD
    mine = small_kernel(
        functools.partial(stack_kernel, columns_of(a_heads)),
        jax.ShapeDtypeStruct((CHIPS, PAGE, width), page.dtype),
        *row_pages,
    )
    other = within_tok(mine, cores=1)

    result = None
    for heads in A_CHUNKS:
        sent = pick_for_rows(tok, served, mine, other)
        pages = across_rows(sent.reshape(ROWS, QB_DEV * PAGE, sent.shape[-1]))
        pages = pages.reshape(DEPTH, QB_DEV, PAGE, sent.shape[-1])
        result = attention(tok, served, (pages,), heads, queries, own_pairs, result)

    sources = chip_copies(level_b)
    own, send = pick_for_pair(tok, served, sources)
    pair = within_tok(send, cores=1)
    result = attention(tok, served, (own, pair), B_HEADS, queries, own_pairs, result)
    return result[None]


def solution(mesh):
    placed = (
        P("section", "tok", None),
        P("section", "tok", None),
        P("section", "tok", None, None),
        P("section", None, None),
    )
    return jax.shard_map(
        on_device, mesh=mesh, in_specs=placed, out_specs=P("section", "tok", None), check_vma=False
    )
```

```python
import functools
import math

import jax
import jax.numpy as jnp
from jax import lax
from jax.experimental import pallas as pl
from jax.experimental.pallas import tpu as pltpu
from jax.sharding import PartitionSpec as P


Q_HEADS = 32
KV_HEADS = 4
GROUP = Q_HEADS // KV_HEADS
HEAD = 128
BLOCK = 128
PAGE = 64
DEPTH = 8
QB_DEV = 2
ROWS, CHIPS, CORES = 8, 4, 2
ROW_DEV = CHIPS * CORES
KEYS = DEPTH * PAGE + BLOCK

A_HEADS = (0, 1)
B_HEADS = (2, 3)


SMEM = functools.partial(pl.BlockSpec, memory_space=pltpu.SMEM)
VMEM = functools.partial(pl.BlockSpec, memory_space=pltpu.VMEM)


def next_section(x):
    n = lax.axis_size("section")
    return lax.ppermute(x, "section", [(i, (i + 1) % n) for i in range(n)])


def within_tok(x, chips=0, cores=0):
    pairs = []
    for row in range(ROWS):
        for chip in range(CHIPS):
            for core in range(CORES):
                there = (row * CHIPS + (chip + chips) % CHIPS) * CORES + (core + cores) % CORES
                pairs.append(((row * CHIPS + chip) * CORES + core, there))
    return lax.ppermute(x, "tok", pairs)


def across_rows(x):
    columns = [[row * ROW_DEV + at for row in range(ROWS)] for at in range(ROW_DEV)]
    return lax.all_to_all(x, "tok", 0, 0, axis_index_groups=columns, tiled=True)


def within_row(x):
    rows = [[row * ROW_DEV + at for at in range(ROW_DEV)] for row in range(ROWS)]
    return lax.all_to_all(x, "tok", 0, 0, axis_index_groups=rows, tiled=True)


def columns_of(heads):
    width = len(heads) * HEAD
    starts = (heads[0] * HEAD, (KV_HEADS + heads[0]) * HEAD)
    return [(i * width, (i + 1) * width, start, start + width) for i, start in enumerate(starts)]


def copies_kernel(columns, page, out):
    for to, to_end, start, end in columns:
        part = page[:, start:end]
        for i in range(out.shape[0]):
            out[i, :, to:to_end] = part


def copies(page, heads, count):
    return pl.pallas_call(
        functools.partial(copies_kernel, columns_of(heads)),
        out_shape=jax.ShapeDtypeStruct((count, PAGE, 2 * len(heads) * HEAD), page.dtype),
        in_specs=[VMEM()],
        out_specs=VMEM(),
        compiler_params=pltpu.CompilerParams(vmem_limit_bytes=4 << 20),
        cost_estimate=pl.CostEstimate(flops=0, transcendentals=0, bytes_accessed=1 << 20),
        name="copies",
    )(page)


def slot_of(served, block, level):
    pick = jnp.clip(served[block, level] - level * ROW_DEV, 0, ROW_DEV - 1)
    return pick >> 1, pick & (CORES - 1)


def place_of(tok):
    return tok >> 3, (tok >> 1) & (CHIPS - 1), tok & (CORES - 1)


def pick_for_rows_kernel(tok, served, pages, out):
    level = tok[0] >> 3
    at = tok[0] & (ROW_DEV - 1)
    for row in range(ROWS):
        for b in range(QB_DEV):
            owner_chip, owner_core = slot_of(served, (row * ROW_DEV + at) * QB_DEV + b, level)
            out[row, b] = pages[owner_chip * CORES + owner_core]


def pick_for_rows(tok, served, pages):
    return pl.pallas_call(
        pick_for_rows_kernel,
        out_shape=jax.ShapeDtypeStruct((ROWS, QB_DEV) + pages.shape[1:], pages.dtype),
        in_specs=[SMEM(), SMEM(), VMEM()],
        out_specs=VMEM(),
        compiler_params=pltpu.CompilerParams(vmem_limit_bytes=16 << 20),
        cost_estimate=pl.CostEstimate(flops=0, transcendentals=0, bytes_accessed=4 << 20),
        name="pick_for_rows",
    )(tok, served, pages)


def pick_for_pair_kernel(tok, served, from0, from1, from2, from3, own, send):
    _, chip, _ = place_of(tok[0])
    for b in range(QB_DEV):
        for level in range(DEPTH):
            for whose, out in ((tok[0], own), (tok[0] ^ 1, send)):
                owner_chip, _ = slot_of(served, whose * QB_DEV + b, level)
                back = (chip - owner_chip) & (CHIPS - 1)
                even = lax.select_n(back == 2, from0[level], from2[level])
                odd = lax.select_n(back == 3, from1[level], from3[level])
                out[b, level] = lax.select_n((back & 1) == 1, even, odd)


def pick_for_pair(tok, served, sources):
    shape = jax.ShapeDtypeStruct((QB_DEV,) + sources[0].shape, sources[0].dtype)
    return pl.pallas_call(
        pick_for_pair_kernel,
        out_shape=(shape, shape),
        in_specs=[SMEM(), SMEM()] + [VMEM()] * CHIPS,
        out_specs=(VMEM(), VMEM()),
        compiler_params=pltpu.CompilerParams(vmem_limit_bytes=16 << 20),
        cost_estimate=pl.CostEstimate(flops=0, transcendentals=0, bytes_accessed=8 << 20),
        name="pick_for_pair",
    )(tok, served, *sources)


def attend(queries, own_keys, own_values, out, keys, values):
    keys[DEPTH * PAGE :, :] = own_keys[...]
    values[DEPTH * PAGE :, :HEAD] = own_values[...]
    values[DEPTH * PAGE :, HEAD:] = jnp.ones((BLOCK, HEAD), jnp.bfloat16)
    to_exp2 = math.log2(math.e) / math.sqrt(HEAD)
    row_index = lax.broadcasted_iota(jnp.int32, (BLOCK, BLOCK), 0)
    col_index = lax.broadcasted_iota(jnp.int32, (BLOCK, BLOCK), 1)
    causal = jnp.where(col_index <= row_index, 0.0, -jnp.inf)
    causal = jnp.concatenate([causal, causal], axis=0)

    def head(g):
        return slice(g * HEAD, (g + 1) * HEAD)

    def score(pair):
        rows = jnp.concatenate([queries[:, head(2 * pair)], queries[:, head(2 * pair + 1)]], axis=0)
        return lax.dot_general(
            rows, keys[...], (((1,), (1,)), ((), ())), preferred_element_type=jnp.float32
        )

    def weigh(scores):
        prefix = scores[:, : DEPTH * PAGE]
        own = scores[:, DEPTH * PAGE :] + causal
        top = jnp.maximum(
            jnp.max(prefix, axis=1, keepdims=True), jnp.max(own, axis=1, keepdims=True)
        )
        parts = [jnp.exp2((part - top) * to_exp2).astype(jnp.bfloat16) for part in (prefix, own)]
        return jnp.concatenate(parts, axis=1)

    def mix(pair, weights):
        mixed = jnp.dot(weights, values[...], preferred_element_type=jnp.float32)
        mixed = (mixed[:, :HEAD] / mixed[:, HEAD:]).astype(out.dtype)
        out[:, head(2 * pair)] = mixed[:BLOCK]
        out[:, head(2 * pair + 1)] = mixed[BLOCK:]

    pairs = GROUP // 2
    scores, weights = score(0), None
    for pair in range(pairs + 1):
        ahead = score(pair + 1) if pair + 1 < pairs else None
        now = weigh(scores) if pair < pairs else None
        if weights is not None:
            mix(pair - 1, weights)
        scores, weights = ahead, now


def attend_kernel(y_first, tok, served, *refs):
    if y_first:
        own_k, own_v, pair_k, pair_v, queries, own_keys, own_values = refs[:7]
    else:
        page_k, page_v, queries, own_keys, own_values = refs[:5]
    out, keys, values = refs[-3:]
    block = tok[0] * QB_DEV + pl.program_id(1)
    core = tok[0] & (CORES - 1)
    first = None
    for level in range(DEPTH):
        if y_first:
            here = slot_of(served, block, level)[1] == core
            key_rows = lax.select_n(here, pair_k[0, level], own_k[0, level])
            value_rows = lax.select_n(here, pair_v[0, level], own_v[0, level])
        else:
            key_rows, value_rows = page_k[level, 0], page_v[level, 0]
        live = served[block, level] >= 0
        first = key_rows if level == 0 else first
        rows = slice(level * PAGE, (level + 1) * PAGE)
        nothing = jnp.zeros((PAGE, HEAD), jnp.bfloat16)
        keys[rows, :] = lax.select_n(live, first, key_rows)
        values[rows, :HEAD] = lax.select_n(live, nothing, value_rows)
        values[rows, HEAD:] = lax.select_n(live, nothing, jnp.ones((PAGE, HEAD), jnp.bfloat16))
    attend(queries, own_keys, own_values, out, keys, values)


def attention(tok, served, pages, heads, queries, pairs, result_heads=None):
    y_first = len(pages) == 2
    queries, queries_at = queries
    pairs, key_at, value_at = pairs
    page_heads, page_at = pages[0].shape[-1] // (2 * HEAD), heads[0]
    count = len(heads)
    if y_first:
        page_block = (1, DEPTH, PAGE, HEAD)
        at = lambda part: pl.BlockSpec(page_block, lambda h, b: (b, 0, 0, part * page_heads + page_at + h))
    else:
        page_block = (DEPTH, 1, PAGE, HEAD)
        at = lambda part: pl.BlockSpec(page_block, lambda h, b: (0, b, 0, part * page_heads + page_at + h))
    block = (BLOCK, GROUP * HEAD)
    own = lambda start: pl.BlockSpec((BLOCK, HEAD), lambda h, b: (b, start + h))
    page_args, page_specs = [], []
    for page in pages:
        page_args += [page, page]
        page_specs += [at(0), at(1)]
    items = count * QB_DEV * GROUP * BLOCK * KEYS
    return pl.pallas_call(
        functools.partial(attend_kernel, y_first),
        grid=(count, QB_DEV),
        out_shape=jax.ShapeDtypeStruct(
            (queries.shape[0], (result_heads or count) * GROUP * HEAD), queries.dtype
        ),
        in_specs=[SMEM(), SMEM()]
        + page_specs
        + [pl.BlockSpec(block, lambda h, b: (b, queries_at + h)), own(key_at), own(value_at)],
        out_specs=pl.BlockSpec(block, lambda h, b: (b, h)),
        scratch_shapes=[
            pltpu.VMEM((KEYS, HEAD), jnp.bfloat16),
            pltpu.VMEM((KEYS, 2 * HEAD), jnp.bfloat16),
        ],
        compiler_params=pltpu.CompilerParams(vmem_limit_bytes=24 << 20),
        cost_estimate=pl.CostEstimate(flops=items * 6 * HEAD, transcendentals=items, bytes_accessed=4 << 20),
        name="attend_b" if y_first else "attend_a",
    )(tok, served, *page_args, queries, pairs, pairs)


def on_device(queries, suffix_kv, prefix_kv, served):
    tok = lax.axis_index("tok").reshape(1)
    queries, suffix_kv, page, served = queries[0], suffix_kv[0], prefix_kv[0, 0], served[0]

    level_b = copies(page, B_HEADS, ROWS)
    level_b = across_rows(level_b)

    page_in = next_section(page)
    served_in = next_section(served)
    queries_in = next_section(queries[:, : len(A_HEADS) * GROUP * HEAD])
    pairs_in = jnp.concatenate(
        [suffix_kv[:, to_start:to_end] for _, _, to_start, to_end in columns_of(A_HEADS)], axis=1
    )
    pairs_in = next_section(pairs_in)

    row_pages = copies(page_in, A_HEADS, ROW_DEV)
    row_pages = within_row(row_pages)
    sent = pick_for_rows(tok, served_in, row_pages)
    pages = across_rows(sent.reshape(ROWS, QB_DEV * PAGE, -1))
    pages = pages.reshape(DEPTH, QB_DEV, PAGE, -1)

    sources = [level_b]
    for d in range(1, CHIPS):
        sources.append(within_tok(level_b, chips=d))
    own, send = pick_for_pair(tok, served, sources)
    pair = within_tok(send, cores=1)
    arrived = []
    for i, h in enumerate(B_HEADS):
        mixed = attention(
            tok, served, (own, pair), (i,), (queries, h), (suffix_kv, h, KV_HEADS + h)
        )
        arrived.append(next_section(mixed))

    result = attention(
        tok, served_in, (pages,), A_HEADS, (queries_in, 0), (pairs_in, 0, len(A_HEADS)), KV_HEADS
    )
    for h, mixed in zip(B_HEADS, arrived):
        result = lax.dynamic_update_slice(result, mixed, (0, h * GROUP * HEAD))
    return result[None]


def solution(mesh):
    placed = (
        P("section", "tok", None),
        P("section", "tok", None),
        P("section", "tok", None, None),
        P("section", None, None),
    )
    return jax.shard_map(
        on_device, mesh=mesh, in_specs=placed, out_specs=P("section", "tok", None), check_vma=False
    )
```

```python
import functools
import math

import jax
import jax.numpy as jnp
from jax import lax
from jax.experimental import pallas as pl
from jax.experimental.pallas import tpu as pltpu
from jax.sharding import PartitionSpec as P


Q_HEADS = 32
KV_HEADS = 4
GROUP = Q_HEADS // KV_HEADS
HEAD = 128
BLOCK = 128
PAGE = 64
DEPTH = 8
QB_DEV = 2
ROWS, CHIPS, CORES = 8, 4, 2
ROW_DEV = CHIPS * CORES
KEYS = DEPTH * PAGE + BLOCK

A_HEADS = (0, 1)
B_HEADS = (2, 3)


SMEM = functools.partial(pl.BlockSpec, memory_space=pltpu.SMEM)
VMEM = functools.partial(pl.BlockSpec, memory_space=pltpu.VMEM)


def next_section(x):
    n = lax.axis_size("section")
    return lax.ppermute(x, "section", [(i, (i + 1) % n) for i in range(n)])


def within_tok(x, chips=0, cores=0):
    pairs = []
    for row in range(ROWS):
        for chip in range(CHIPS):
            for core in range(CORES):
                there = (row * CHIPS + (chip + chips) % CHIPS) * CORES + (core + cores) % CORES
                pairs.append(((row * CHIPS + chip) * CORES + core, there))
    return lax.ppermute(x, "tok", pairs)


def across_rows(x):
    columns = [[row * ROW_DEV + at for row in range(ROWS)] for at in range(ROW_DEV)]
    return lax.all_to_all(x, "tok", 0, 0, axis_index_groups=columns, tiled=True)


def columns_of(heads):
    width = len(heads) * HEAD
    starts = (heads[0] * HEAD, (KV_HEADS + heads[0]) * HEAD)
    return [(i * width, (i + 1) * width, start, start + width) for i, start in enumerate(starts)]


def copies_kernel(columns, page, out):
    for to, to_end, start, end in columns:
        part = page[:, start:end]
        for i in range(out.shape[0]):
            out[i, :, to:to_end] = part


def stack_kernel(columns, *refs):
    out = refs[-1]
    for i, page in enumerate(refs[:-1]):
        for to, to_end, start, end in columns:
            out[i, :, to:to_end] = page[:, start:end]


def small_kernel(body, out_shape, *args):
    return pl.pallas_call(
        body,
        out_shape=out_shape,
        in_specs=[VMEM()] * len(args),
        out_specs=VMEM(),
        compiler_params=pltpu.CompilerParams(vmem_limit_bytes=4 << 20),
        cost_estimate=pl.CostEstimate(flops=0, transcendentals=0, bytes_accessed=1 << 20),
    )(*args)


def slot_of(served, block, level):
    pick = jnp.clip(served[block, level] - level * ROW_DEV, 0, ROW_DEV - 1)
    return pick >> 1, pick & (CORES - 1)


def place_of(tok):
    return tok >> 3, (tok >> 1) & (CHIPS - 1), tok & (CORES - 1)


def pick_for_rows_kernel(tok, served, mine, other, out):
    level, chip, core = place_of(tok[0])
    at = tok[0] & (ROW_DEV - 1)
    for row in range(ROWS):
        for b in range(QB_DEV):
            owner_chip, owner_core = slot_of(served, (row * ROW_DEV + at) * QB_DEV + b, level)
            back = (chip - owner_chip) & (CHIPS - 1)
            out[row, b] = lax.select_n(owner_core == core, other[back], mine[back])


def pick_for_rows(tok, served, mine, other):
    width = mine.shape[-1]
    return pl.pallas_call(
        pick_for_rows_kernel,
        out_shape=jax.ShapeDtypeStruct((ROWS, QB_DEV, PAGE, width), mine.dtype),
        in_specs=[SMEM(), SMEM(), VMEM(), VMEM()],
        out_specs=VMEM(),
        compiler_params=pltpu.CompilerParams(vmem_limit_bytes=16 << 20),
        cost_estimate=pl.CostEstimate(flops=0, transcendentals=0, bytes_accessed=4 << 20),
        name="pick_for_rows",
    )(tok, served, mine, other)


def pick_for_pair_kernel(tok, served, from0, from1, from2, from3, own, send):
    _, chip, _ = place_of(tok[0])
    for b in range(QB_DEV):
        for level in range(DEPTH):
            for whose, out in ((tok[0], own), (tok[0] ^ 1, send)):
                owner_chip, _ = slot_of(served, whose * QB_DEV + b, level)
                back = (chip - owner_chip) & (CHIPS - 1)
                even = lax.select_n(back == 2, from0[level], from2[level])
                odd = lax.select_n(back == 3, from1[level], from3[level])
                out[b, level] = lax.select_n((back & 1) == 1, even, odd)


def pick_for_pair(tok, served, sources):
    shape = jax.ShapeDtypeStruct((QB_DEV,) + sources[0].shape, sources[0].dtype)
    return pl.pallas_call(
        pick_for_pair_kernel,
        out_shape=(shape, shape),
        in_specs=[SMEM(), SMEM()] + [VMEM()] * CHIPS,
        out_specs=(VMEM(), VMEM()),
        compiler_params=pltpu.CompilerParams(vmem_limit_bytes=16 << 20),
        cost_estimate=pl.CostEstimate(flops=0, transcendentals=0, bytes_accessed=8 << 20),
        name="pick_for_pair",
    )(tok, served, *sources)


def attend(queries, own_keys, own_values, out, keys, values):
    keys[DEPTH * PAGE :, :] = own_keys[...]
    values[DEPTH * PAGE :, :HEAD] = own_values[...]
    values[DEPTH * PAGE :, HEAD:] = jnp.ones((BLOCK, HEAD), jnp.bfloat16)
    to_exp2 = math.log2(math.e) / math.sqrt(HEAD)
    row_index = lax.broadcasted_iota(jnp.int32, (BLOCK, BLOCK), 0)
    col_index = lax.broadcasted_iota(jnp.int32, (BLOCK, BLOCK), 1)
    causal = jnp.where(col_index <= row_index, 0.0, -jnp.inf)
    causal = jnp.concatenate([causal, causal], axis=0)

    def head(g):
        return slice(g * HEAD, (g + 1) * HEAD)

    def score(pair):
        rows = jnp.concatenate([queries[:, head(2 * pair)], queries[:, head(2 * pair + 1)]], axis=0)
        return lax.dot_general(
            rows, keys[...], (((1,), (1,)), ((), ())), preferred_element_type=jnp.float32
        )

    def weigh(scores):
        prefix = scores[:, : DEPTH * PAGE]
        own = scores[:, DEPTH * PAGE :] + causal
        top = jnp.maximum(
            jnp.max(prefix, axis=1, keepdims=True), jnp.max(own, axis=1, keepdims=True)
        )
        parts = [jnp.exp2((part - top) * to_exp2).astype(jnp.bfloat16) for part in (prefix, own)]
        return jnp.concatenate(parts, axis=1)

    def mix(pair, weights):
        mixed = jnp.dot(weights, values[...], preferred_element_type=jnp.float32)
        mixed = (mixed[:, :HEAD] / mixed[:, HEAD:]).astype(out.dtype)
        out[:, head(2 * pair)] = mixed[:BLOCK]
        out[:, head(2 * pair + 1)] = mixed[BLOCK:]

    pairs = GROUP // 2
    scores, weights = score(0), None
    for pair in range(pairs + 1):
        ahead = score(pair + 1) if pair + 1 < pairs else None
        now = weigh(scores) if pair < pairs else None
        if weights is not None:
            mix(pair - 1, weights)
        scores, weights = ahead, now


def attend_kernel(y_first, tok, served, *refs):
    if y_first:
        own_k, own_v, pair_k, pair_v, queries, own_keys, own_values = refs[:7]
    else:
        page_k, page_v, queries, own_keys, own_values = refs[:5]
    out, keys, values = refs[-3:]
    block = tok[0] * QB_DEV + pl.program_id(1)
    core = tok[0] & (CORES - 1)
    first = None
    for level in range(DEPTH):
        if y_first:
            here = slot_of(served, block, level)[1] == core
            key_rows = lax.select_n(here, pair_k[0, level], own_k[0, level])
            value_rows = lax.select_n(here, pair_v[0, level], own_v[0, level])
        else:
            key_rows, value_rows = page_k[level, 0], page_v[level, 0]
        live = served[block, level] >= 0
        first = key_rows if level == 0 else first
        rows = slice(level * PAGE, (level + 1) * PAGE)
        nothing = jnp.zeros((PAGE, HEAD), jnp.bfloat16)
        keys[rows, :] = lax.select_n(live, first, key_rows)
        values[rows, :HEAD] = lax.select_n(live, nothing, value_rows)
        values[rows, HEAD:] = lax.select_n(live, nothing, jnp.ones((PAGE, HEAD), jnp.bfloat16))
    attend(queries, own_keys, own_values, out, keys, values)


def attention(tok, served, pages, heads, queries, own_pairs, result):
    y_first = len(pages) == 2
    count, first = len(heads), heads[0]
    if y_first:
        page_block = (1, DEPTH, PAGE, HEAD)
        at = lambda part: pl.BlockSpec(page_block, lambda h, b: (b, 0, 0, part * count + h))
    else:
        page_block = (DEPTH, 1, PAGE, HEAD)
        at = lambda part: pl.BlockSpec(page_block, lambda h, b: (0, b, 0, part * count + h))
    wide = pl.BlockSpec((BLOCK, GROUP * HEAD), lambda h, b: (b, first + h))
    own = lambda part: pl.BlockSpec((BLOCK, HEAD), lambda h, b: (b, part * KV_HEADS + first + h))
    page_args, page_specs = [], []
    for page in pages:
        page_args += [page, page]
        page_specs += [at(0), at(1)]
    args = [tok, served] + page_args + [queries, own_pairs, own_pairs]
    specs = [SMEM(), SMEM()] + page_specs + [wide, own(0), own(1)]
    aliases = {}
    if result is not None:
        aliases = {len(args): 0}
        args.append(result)
        specs.append(pl.BlockSpec(memory_space=pl.ANY))
    items = count * QB_DEV * GROUP * BLOCK * KEYS
    return pl.pallas_call(
        functools.partial(attend_kernel, y_first),
        grid=(count, QB_DEV),
        out_shape=jax.ShapeDtypeStruct(queries.shape, queries.dtype),
        in_specs=specs,
        out_specs=wide,
        scratch_shapes=[pltpu.VMEM((KEYS, HEAD), jnp.bfloat16), pltpu.VMEM((KEYS, 2 * HEAD), jnp.bfloat16)],
        input_output_aliases=aliases,
        compiler_params=pltpu.CompilerParams(vmem_limit_bytes=24 << 20),
        cost_estimate=pl.CostEstimate(flops=items * 6 * HEAD, transcendentals=items, bytes_accessed=4 << 20),
        name="attend_b" if y_first else "attend_a",
    )(*args)


def on_device(queries, suffix_kv, prefix_kv, served):
    tok = lax.axis_index("tok").reshape(1)
    page = next_section(prefix_kv[0, 0])
    served = next_section(served[0])
    own_pairs = next_section(suffix_kv[0])
    queries = next_section(queries[0])

    def chip_copies(x):
        copies = [x]
        for d in range(1, CHIPS):
            copies.append(within_tok(x, chips=d))
        return copies

    width = 2 * len(B_HEADS) * HEAD
    level_b = small_kernel(
        functools.partial(copies_kernel, columns_of(B_HEADS)),
        jax.ShapeDtypeStruct((ROWS, PAGE, width), page.dtype),
        page,
    )
    level_b = across_rows(level_b)

    row_pages = chip_copies(page)
    width = 2 * len(A_HEADS) * HEAD
    mine = small_kernel(
        functools.partial(stack_kernel, columns_of(A_HEADS)),
        jax.ShapeDtypeStruct((CHIPS, PAGE, width), page.dtype),
        *row_pages,
    )
    other = within_tok(mine, cores=1)

    sent = pick_for_rows(tok, served, mine, other)
    pages = across_rows(sent.reshape(ROWS, QB_DEV * PAGE, width))
    pages = pages.reshape(DEPTH, QB_DEV, PAGE, width)

    sources = chip_copies(level_b)
    own, send = pick_for_pair(tok, served, sources)
    pair = within_tok(send, cores=1)
    result = attention(tok, served, (own, pair), B_HEADS, queries, own_pairs, None)
    result = attention(tok, served, (pages,), A_HEADS, queries, own_pairs, result)
    return result[None]


def solution(mesh):
    placed = (
        P("section", "tok", None),
        P("section", "tok", None),
        P("section", "tok", None, None),
        P("section", None, None),
    )
    return jax.shard_map(
        on_device, mesh=mesh, in_specs=placed, out_specs=P("section", "tok", None), check_vma=False
    )
```

```python
import functools
import math

import jax
import jax.numpy as jnp
from jax import lax
from jax.experimental import pallas as pl
from jax.experimental.pallas import tpu as pltpu
from jax.sharding import PartitionSpec as P


Q_HEADS = 32
KV_HEADS = 4
GROUP = Q_HEADS // KV_HEADS
HEAD = 128
BLOCK = 128
PAGE = 64
DEPTH = 8
QB_DEV = 2
ROWS, CHIPS, CORES = 8, 4, 2
ROW_DEV = CHIPS * CORES
KEYS = DEPTH * PAGE + BLOCK

A_HEADS = (0, 1)
B_HEADS = (2, 3)


SMEM = functools.partial(pl.BlockSpec, memory_space=pltpu.SMEM)
VMEM = functools.partial(pl.BlockSpec, memory_space=pltpu.VMEM)


def next_section(x):
    n = lax.axis_size("section")
    return lax.ppermute(x, "section", [(i, (i + 1) % n) for i in range(n)])


def within_tok(x, chips=0, cores=0):
    pairs = []
    for row in range(ROWS):
        for chip in range(CHIPS):
            for core in range(CORES):
                there = (row * CHIPS + (chip + chips) % CHIPS) * CORES + (core + cores) % CORES
                pairs.append(((row * CHIPS + chip) * CORES + core, there))
    return lax.ppermute(x, "tok", pairs)


def across_rows(x):
    columns = [[row * ROW_DEV + at for row in range(ROWS)] for at in range(ROW_DEV)]
    return lax.all_to_all(x, "tok", 0, 0, axis_index_groups=columns, tiled=True)


def columns_of(heads):
    width = len(heads) * HEAD
    starts = (heads[0] * HEAD, (KV_HEADS + heads[0]) * HEAD)
    return [(i * width, (i + 1) * width, start, start + width) for i, start in enumerate(starts)]


def copies_kernel(columns, page, out):
    for to, to_end, start, end in columns:
        part = page[:, start:end]
        for i in range(out.shape[0]):
            out[i, :, to:to_end] = part


def stack_kernel(columns, *refs):
    out = refs[-1]
    for i, page in enumerate(refs[:-1]):
        for to, to_end, start, end in columns:
            out[i, :, to:to_end] = page[:, start:end]


def small_kernel(body, out_shape, *args):
    return pl.pallas_call(
        body,
        out_shape=out_shape,
        in_specs=[VMEM()] * len(args),
        out_specs=VMEM(),
        compiler_params=pltpu.CompilerParams(vmem_limit_bytes=4 << 20),
        cost_estimate=pl.CostEstimate(flops=0, transcendentals=0, bytes_accessed=1 << 20),
    )(*args)


def slot_of(served, block, level):
    pick = jnp.clip(served[block, level] - level * ROW_DEV, 0, ROW_DEV - 1)
    return pick >> 1, pick & (CORES - 1)


def place_of(tok):
    return tok >> 3, (tok >> 1) & (CHIPS - 1), tok & (CORES - 1)


def pick_for_rows_kernel(tok, served, mine, other, out):
    level, chip, core = place_of(tok[0])
    at = tok[0] & (ROW_DEV - 1)
    for row in range(ROWS):
        for b in range(QB_DEV):
            owner_chip, owner_core = slot_of(served, (row * ROW_DEV + at) * QB_DEV + b, level)
            back = (chip - owner_chip) & (CHIPS - 1)
            out[row, b] = lax.select_n(owner_core == core, other[back], mine[back])


def pick_for_rows(tok, served, mine, other):
    width = mine.shape[-1]
    return pl.pallas_call(
        pick_for_rows_kernel,
        out_shape=jax.ShapeDtypeStruct((ROWS, QB_DEV, PAGE, width), mine.dtype),
        in_specs=[SMEM(), SMEM(), VMEM(), VMEM()],
        out_specs=VMEM(),
        compiler_params=pltpu.CompilerParams(vmem_limit_bytes=16 << 20),
        cost_estimate=pl.CostEstimate(flops=0, transcendentals=0, bytes_accessed=4 << 20),
        name="pick_for_rows",
    )(tok, served, mine, other)


def pick_for_pair_kernel(tok, served, from0, from1, from2, from3, own, send):
    _, chip, _ = place_of(tok[0])
    for b in range(QB_DEV):
        for level in range(DEPTH):
            for whose, out in ((tok[0], own), (tok[0] ^ 1, send)):
                owner_chip, _ = slot_of(served, whose * QB_DEV + b, level)
                back = (chip - owner_chip) & (CHIPS - 1)
                even = lax.select_n(back == 2, from0[level], from2[level])
                odd = lax.select_n(back == 3, from1[level], from3[level])
                out[b, level] = lax.select_n((back & 1) == 1, even, odd)


def pick_for_pair(tok, served, sources):
    shape = jax.ShapeDtypeStruct((QB_DEV,) + sources[0].shape, sources[0].dtype)
    return pl.pallas_call(
        pick_for_pair_kernel,
        out_shape=(shape, shape),
        in_specs=[SMEM(), SMEM()] + [VMEM()] * CHIPS,
        out_specs=(VMEM(), VMEM()),
        compiler_params=pltpu.CompilerParams(vmem_limit_bytes=16 << 20),
        cost_estimate=pl.CostEstimate(flops=0, transcendentals=0, bytes_accessed=8 << 20),
        name="pick_for_pair",
    )(tok, served, *sources)


def attend(queries, own_keys, own_values, out, keys, values):
    keys[DEPTH * PAGE :, :] = own_keys[...]
    values[DEPTH * PAGE :, :HEAD] = own_values[...]
    values[DEPTH * PAGE :, HEAD:] = jnp.ones((BLOCK, HEAD), jnp.bfloat16)
    to_exp2 = math.log2(math.e) / math.sqrt(HEAD)
    row_index = lax.broadcasted_iota(jnp.int32, (BLOCK, BLOCK), 0)
    col_index = lax.broadcasted_iota(jnp.int32, (BLOCK, BLOCK), 1)
    causal = jnp.where(col_index <= row_index, 0.0, -jnp.inf)
    causal = jnp.concatenate([causal, causal], axis=0)

    def head(g):
        return slice(g * HEAD, (g + 1) * HEAD)

    def score(pair):
        rows = jnp.concatenate([queries[:, head(2 * pair)], queries[:, head(2 * pair + 1)]], axis=0)
        return lax.dot_general(
            rows, keys[...], (((1,), (1,)), ((), ())), preferred_element_type=jnp.float32
        )

    def weigh(scores):
        prefix = scores[:, : DEPTH * PAGE]
        own = scores[:, DEPTH * PAGE :] + causal
        top = jnp.maximum(
            jnp.max(prefix, axis=1, keepdims=True), jnp.max(own, axis=1, keepdims=True)
        )
        parts = [jnp.exp2((part - top) * to_exp2).astype(jnp.bfloat16) for part in (prefix, own)]
        return jnp.concatenate(parts, axis=1)

    def mix(pair, weights):
        mixed = jnp.dot(weights, values[...], preferred_element_type=jnp.float32)
        mixed = (mixed[:, :HEAD] / mixed[:, HEAD:]).astype(out.dtype)
        out[:, head(2 * pair)] = mixed[:BLOCK]
        out[:, head(2 * pair + 1)] = mixed[BLOCK:]

    pairs = GROUP // 2
    scores, weights = score(0), None
    for pair in range(pairs + 1):
        ahead = score(pair + 1) if pair + 1 < pairs else None
        now = weigh(scores) if pair < pairs else None
        if weights is not None:
            mix(pair - 1, weights)
        scores, weights = ahead, now


def attend_kernel(heads, y_first, tok, served, *refs):
    pages, (queries, pairs) = refs[: 1 + y_first], refs[1 + y_first : 3 + y_first]
    out, keys, values = refs[-3:]
    count, first_head = len(heads), heads[0]
    h, b = pl.program_id(0), pl.program_id(1)
    block = tok[0] * QB_DEV + b
    core = tok[0] & (CORES - 1)

    def columns(start, width=HEAD):
        return pl.ds(pl.multiple_of(start * width, width), width)

    def page_rows(level, part):
        at = columns(part * count + h)
        if not y_first:
            return pages[0][level, b, :, at]
        here = slot_of(served, block, level)[1] == core
        return lax.select_n(here, pages[1][b, level, :, at], pages[0][b, level, :, at])

    first = None
    for level in range(DEPTH):
        key_rows, value_rows = page_rows(level, 0), page_rows(level, 1)
        live = served[block, level] >= 0
        first = key_rows if level == 0 else first
        rows = slice(level * PAGE, (level + 1) * PAGE)
        nothing = jnp.zeros((PAGE, HEAD), jnp.bfloat16)
        keys[rows, :] = lax.select_n(live, first, key_rows)
        values[rows, :HEAD] = lax.select_n(live, nothing, value_rows)
        values[rows, HEAD:] = lax.select_n(live, nothing, jnp.ones((PAGE, HEAD), jnp.bfloat16))
    own = pl.ds(pl.multiple_of(b * BLOCK, BLOCK), BLOCK)
    attend(
        queries.at[own, columns(first_head + h, GROUP * HEAD)],
        pairs.at[own, columns(first_head + h)],
        pairs.at[own, columns(KV_HEADS + first_head + h)],
        out,
        keys,
        values,
    )


def attention(tok, served, pages, heads, queries, own_pairs, result):
    y_first = len(pages) == 2
    args = [tok, served, *pages, queries, own_pairs]
    specs = [SMEM(), SMEM()] + [VMEM()] * (len(args) - 2)
    aliases = {}
    if result is not None:
        aliases = {len(args): 0}
        args.append(result)
        specs.append(pl.BlockSpec(memory_space=pl.ANY))
    items = len(heads) * QB_DEV * GROUP * BLOCK * KEYS
    return pl.pallas_call(
        functools.partial(attend_kernel, heads, y_first),
        grid=(len(heads), QB_DEV),
        out_shape=jax.ShapeDtypeStruct(queries.shape, queries.dtype),
        in_specs=specs,
        out_specs=pl.BlockSpec((BLOCK, GROUP * HEAD), lambda h, b: (b, heads[0] + h)),
        scratch_shapes=[
            pltpu.VMEM((KEYS, HEAD), jnp.bfloat16),
            pltpu.VMEM((KEYS, 2 * HEAD), jnp.bfloat16),
        ],
        input_output_aliases=aliases,
        compiler_params=pltpu.CompilerParams(vmem_limit_bytes=24 << 20),
        cost_estimate=pl.CostEstimate(flops=items * 6 * HEAD, transcendentals=items, bytes_accessed=4 << 20),
        name="attend_b" if y_first else "attend_a",
    )(*args)


def on_device(queries, suffix_kv, prefix_kv, served):
    tok = lax.axis_index("tok").reshape(1)
    page = next_section(prefix_kv[0, 0])
    served = next_section(served[0])
    own_pairs = next_section(suffix_kv[0])
    queries = next_section(queries[0])

    def chip_copies(x):
        copies = [x]
        for d in range(1, CHIPS):
            copies.append(within_tok(x, chips=d))
        return copies

    width = 2 * len(B_HEADS) * HEAD
    level_b = small_kernel(
        functools.partial(copies_kernel, columns_of(B_HEADS)),
        jax.ShapeDtypeStruct((ROWS, PAGE, width), page.dtype),
        page,
    )
    level_b = across_rows(level_b)

    row_pages = chip_copies(page)
    width = 2 * len(A_HEADS) * HEAD
    mine = small_kernel(
        functools.partial(stack_kernel, columns_of(A_HEADS)),
        jax.ShapeDtypeStruct((CHIPS, PAGE, width), page.dtype),
        *row_pages,
    )
    other = within_tok(mine, cores=1)

    sent = pick_for_rows(tok, served, mine, other)
    pages = across_rows(sent.reshape(ROWS, QB_DEV * PAGE, width))
    pages = pages.reshape(DEPTH, QB_DEV, PAGE, width)

    sources = chip_copies(level_b)
    own, send = pick_for_pair(tok, served, sources)
    pair = within_tok(send, cores=1)
    result = attention(tok, served, (own, pair), B_HEADS, queries, own_pairs, None)
    result = attention(tok, served, (pages,), A_HEADS, queries, own_pairs, result)
    return result[None]


def solution(mesh):
    placed = (
        P("section", "tok", None),
        P("section", "tok", None),
        P("section", "tok", None, None),
        P("section", None, None),
    )
    return jax.shard_map(
        on_device, mesh=mesh, in_specs=placed, out_specs=P("section", "tok", None), check_vma=False
    )
```
